256 devices in a mesh: seq: 64 (over y, z, core), head: 4 (over x).
Axes of the slice: x: 4, y: 4, z: 8, core: 2. Of those that a mesh axis runs over, the one named last changes fastest.
Arguments:
- queries: bfloat16 [65536, 4, 512], P(('seq', 'head')), may hold values from -12 to 12
- key_value: bfloat16 [65536, 4, 256], P(('seq', 'head')), may hold values from -5 to 5
- rand_blocks: int32 [256, 16, 3], replicated, may hold values from 0 to 255, as said below
Outputs:
- attended: bfloat16 [65536, 4, 512], P('seq', 'head')
The draws below stay inside these ranges and needn't reach their ends.
Inputs may be any that keep to these rules, and one draw needn't show every extreme that they name: Block c is held by index c // 4 of seq. For each key-value head a and each aligned run of 4 query blocks, the 48 entries rand_blocks[c, a * 4 + g, :] of those blocks name blocks of any one holder at most 1 times, counted with repeats, and some holder exactly 1 times.
All inputs are finite; a program needn't handle non-finite values.
Results may differ from the reference program's by a relative error of at most 0.0039.
Values may be sent and summed in bfloat16 or wider, within the bound.
A program may use at most 192 MiB of HBM per device.

```python
import jax
import jax.numpy as jnp
from jax import lax

HD = 128
KVH = 4
QH = 16
BLOCK = 256
BLK_DEV = 4
GROUP = 4
NBLK = 256
TOKENS = 65536
N_SEQ = 64


def draw_queries(key, part):
    own_key = jax.random.fold_in(key, 1)
    array_shape = (TOKENS, KVH, GROUP * HD)
    values = jnp.clip(3.0 * jax.random.normal(own_key, array_shape, jnp.float32), -12.0, 12.0)
    return values.astype(jnp.bfloat16)


def draw_key_value(key, part):
    own_key = jax.random.fold_in(key, 2)
    array_shape = (TOKENS, KVH, 2 * HD)
    values = jnp.clip(jax.random.normal(own_key, array_shape, jnp.float32), -5.0, 5.0)
    return values.astype(jnp.bfloat16)


def draw_rand_blocks(key, part):
    slot_count = 3 * GROUP * BLK_DEV

    def per_reader(reader_head):
        reader_key = jax.random.fold_in(key, reader_head)
        holder_order = jax.random.permutation(jax.random.fold_in(reader_key, 1), N_SEQ)
        sources = holder_order[jnp.arange(slot_count) % N_SEQ]
        within = jax.random.randint(jax.random.fold_in(reader_key, 2), (slot_count,), 0, BLK_DEV)
        blocks = sources * BLK_DEV + within
        shuffle = jax.random.permutation(jax.random.fold_in(reader_key, 3), slot_count)
        return blocks[shuffle].reshape(BLK_DEV, GROUP, 3)
    listed = jax.vmap(per_reader)(jnp.arange(N_SEQ * KVH))
    listed = listed.reshape(N_SEQ, KVH, BLK_DEV, GROUP, 3).transpose(0, 2, 1, 3, 4)
    return listed.reshape(NBLK, QH, 3).astype(jnp.int32)


def setup_inputs(seed: int = 0) -> dict:
    seeds = jax.random.split(jax.random.key(seed), 4)
    queries = draw_queries(jax.random.fold_in(seeds[3], 71), 0)
    key_value = draw_key_value(jax.random.fold_in(seeds[3], 71), 0)
    rand_blocks = draw_rand_blocks(jax.random.fold_in(seeds[3], 71), 0)
    return {"queries": queries, "key_value": key_value, "rand_blocks": rand_blocks}


def reference(queries, key_value, rand_blocks):
    score_scale = HD ** -0.5
    levels = NBLK.bit_length() - 1
    query_blocks = queries.reshape(NBLK, BLOCK, KVH, GROUP, HD)
    pair_blocks = key_value.reshape(NBLK, BLOCK, KVH, 2 * HD)
    flip_masks = jnp.array([1 << level for level in range(levels)], dtype=jnp.int32)
    head_index = jnp.arange(KVH, dtype=jnp.int32)[:, None, None]
    shared_count = 1 + levels

    def one_block(block_index):
        listed = jnp.concatenate([block_index[None], jnp.bitwise_xor(block_index, flip_masks)]).astype(jnp.int32)
        chosen = pair_blocks[listed].astype(jnp.float32)
        rand_here = rand_blocks[block_index].reshape(KVH, GROUP, 3).astype(jnp.int32)
        picked = pair_blocks[rand_here, :, head_index].astype(jnp.float32)
        query_block = query_blocks[block_index].astype(jnp.float32)
        shared_scores = jnp.einsum("qkgd,jukd->jqkgu", query_block, chosen[..., :HD])
        rand_scores = jnp.einsum("qkgd,kgrud->rqkgu", query_block, picked[..., :HD])
        scores = jnp.concatenate([shared_scores, rand_scores], axis=0) * score_scale
        block_max = jnp.max(scores, axis=-1)
        weights = jnp.exp(scores - block_max[..., None]).astype(jnp.bfloat16)
        weights = lax.optimization_barrier(weights).astype(jnp.float32)
        totals = jnp.sum(weights, axis=-1)
        shared_part = jnp.einsum("jqkgu,jukd->jqkgd", weights[:shared_count], chosen[..., HD:])
        rand_part = jnp.einsum("rqkgu,kgrud->rqkgd", weights[shared_count:], picked[..., HD:])
        partial_value = jnp.concatenate([shared_part, rand_part], axis=0)
        highest = jnp.max(block_max, axis=0)
        factor = jnp.exp(block_max - highest)
        numer = jnp.sum(factor[..., None] * partial_value, axis=0)
        denom = jnp.sum(factor * totals, axis=0)
        return (numer / denom[..., None]).astype(jnp.bfloat16)

    attended = lax.map(one_block, jnp.arange(NBLK, dtype=jnp.int32))
    return attended.reshape(TOKENS, KVH, GROUP * HD)
```

```python
import jax
import jax.numpy as jnp
import numpy as np
from jax import lax
from jax.experimental import pallas as pl
from jax.experimental.pallas import tpu as pltpu
from jax.sharding import PartitionSpec as P

HD = 128
BLOCK = 256
LISTED = 21
SHARED = 9


def attend_kernel(table, q_ref, kv_ref, o_ref, kbuf, vbuf, sem):
    c = pl.program_id(0)
    slot = c % 2

    def copies(step, where):
        made = []
        for j in range(LISTED):
            block = table[step * LISTED + j]
            made.append(pltpu.make_async_copy(
                kv_ref.at[block, :, 0:HD], kbuf.at[where, pl.ds(j * BLOCK, BLOCK)], sem.at[where, 0, j]))
            made.append(pltpu.make_async_copy(
                kv_ref.at[block, :, HD:2 * HD], vbuf.at[where, pl.ds(j * BLOCK, BLOCK), 0:HD], sem.at[where, 1, j]))
        return made

    @pl.when(c == 0)
    def _():
        for copy in copies(0, 0):
            copy.start()
        vbuf[:, :, HD:2 * HD] = jnp.ones((2, LISTED * BLOCK, HD), jnp.bfloat16)

    @pl.when(c + 1 < pl.num_programs(0))
    def _():
        for copy in copies(c + 1, 1 - slot):
            copy.start()

    for copy in copies(c, slot):
        copy.wait()
    factor = HD ** (-0.5) * np.log2(np.e)
    for g in range(4):
        q = q_ref[:, g * HD:(g + 1) * HD]
        nt = (((1,), (1,)), ((), ()))
        lo = SHARED * BLOCK
        ro = (SHARED + 3 * g) * BLOCK
        s1 = lax.dot_general(q, kbuf[slot, 0:lo], nt, preferred_element_type=jnp.float32)
        s2 = lax.dot_general(q, kbuf[slot, ro:ro + 3 * BLOCK], nt, preferred_element_type=jnp.float32)
        m = jnp.maximum(jnp.max(s1, axis=-1, keepdims=True), jnp.max(s2, axis=-1, keepdims=True))
        p1 = jnp.exp2((s1 - m) * factor).astype(jnp.bfloat16)
        p2 = jnp.exp2((s2 - m) * factor).astype(jnp.bfloat16)
        o = jnp.dot(p1, vbuf[slot, 0:lo], preferred_element_type=jnp.float32)
        o += jnp.dot(p2, vbuf[slot, ro:ro + 3 * BLOCK], preferred_element_type=jnp.float32)
        o_ref[:, g * HD:(g + 1) * HD] = (o[:, :HD] / o[:, HD:]).astype(jnp.bfloat16)


def on_device(queries, key_value, rand_blocks):
    q = lax.all_to_all(queries, "head", split_axis=1, concat_axis=0, tiled=True).reshape(1024, 512)
    kv = lax.all_to_all(key_value, "head", split_axis=1, concat_axis=0, tiled=True).reshape(4, BLOCK, 2 * HD)
    seq = lax.axis_index("seq")
    head = lax.axis_index("head")
    kv_all = lax.all_gather(kv, "seq", axis=0, tiled=True)
    blocks = seq * 4 + jnp.arange(4, dtype=jnp.int32)
    flips = jnp.array([0] + [1 << i for i in range(8)], dtype=jnp.int32)
    shared = blocks[:, None] ^ flips[None]
    mine = lax.dynamic_slice(rand_blocks, (seq * 4, head * 4, 0), (4, 4, 3)).reshape(4, 12)
    table = jnp.concatenate([shared, mine], axis=1).reshape(-1).astype(jnp.int32)
    out = pl.pallas_call(
        attend_kernel,
        grid_spec=pltpu.PrefetchScalarGridSpec(
            num_scalar_prefetch=1, grid=(4,),
            in_specs=[pl.BlockSpec((BLOCK, 4 * HD), lambda c, t: (c, 0)),
                      pl.BlockSpec(memory_space=pl.ANY)],
            out_specs=pl.BlockSpec((BLOCK, 4 * HD), lambda c, t: (c, 0)),
            scratch_shapes=[pltpu.VMEM((2, LISTED * BLOCK, HD), jnp.bfloat16),
                            pltpu.VMEM((2, LISTED * BLOCK, 2 * HD), jnp.bfloat16),
                            pltpu.SemaphoreType.DMA((2, 2, LISTED))]),
        out_shape=jax.ShapeDtypeStruct((1024, 512), jnp.bfloat16),
        compiler_params=pltpu.CompilerParams(dimension_semantics=("arbitrary",), vmem_limit_bytes=60 << 20),
        name="attend",
    )(table, q, kv_all)
    return out.reshape(1024, 1, 512)


def solution(mesh):
    in_specs = (P(("seq", "head"), None, None), P(("seq", "head"), None, None), P())
    return jax.shard_map(on_device, mesh=mesh, in_specs=in_specs, out_specs=P("seq", "head", None), check_vma=False)
```

```python
import jax
import jax.numpy as jnp
import numpy as np
from jax import lax
from jax.experimental import pallas as pl
from jax.experimental.pallas import tpu as pltpu
from jax.sharding import PartitionSpec as P

HD = 128
BLOCK = 256
LISTED = 21
SHARED = 9


def attend_kernel(table, q_ref, kv_ref, o_ref, kbuf, vbuf, sem):
    c = pl.program_id(0)
    slot = c % 2

    def copies(step, where):
        made = []
        for j in range(LISTED):
            block = table[step * LISTED + j]
            made.append(pltpu.make_async_copy(
                kv_ref.at[block, :, 0:HD], kbuf.at[where, pl.ds(j * BLOCK, BLOCK)], sem.at[where, 0, j]))
            made.append(pltpu.make_async_copy(
                kv_ref.at[block, :, HD:2 * HD], vbuf.at[where, pl.ds(j * BLOCK, BLOCK), 0:HD], sem.at[where, 1, j]))
        return made

    @pl.when(c == 0)
    def _():
        for copy in copies(0, 0):
            copy.start()
        vbuf[:, :, HD:2 * HD] = jnp.ones((2, LISTED * BLOCK, HD), jnp.bfloat16)

    @pl.when(c + 1 < pl.num_programs(0))
    def _():
        for copy in copies(c + 1, 1 - slot):
            copy.start()

    for copy in copies(c, slot):
        copy.wait()
    factor = HD ** (-0.5) * np.log2(np.e)
    for g in range(4):
        q = q_ref[:, g * HD:(g + 1) * HD]
        nt = (((1,), (1,)), ((), ()))
        lo = SHARED * BLOCK
        ro = (SHARED + 3 * g) * BLOCK
        s1 = lax.dot_general(q, kbuf[slot, 0:lo], nt, preferred_element_type=jnp.float32)
        s2 = lax.dot_general(q, kbuf[slot, ro:ro + 3 * BLOCK], nt, preferred_element_type=jnp.float32)
        m = jnp.maximum(jnp.max(s1, axis=-1, keepdims=True), jnp.max(s2, axis=-1, keepdims=True))
        p1 = jnp.exp2((s1 - m) * factor).astype(jnp.bfloat16)
        p2 = jnp.exp2((s2 - m) * factor).astype(jnp.bfloat16)
        o = jnp.dot(p1, vbuf[slot, 0:lo], preferred_element_type=jnp.float32)
        o += jnp.dot(p2, vbuf[slot, ro:ro + 3 * BLOCK], preferred_element_type=jnp.float32)
        o_ref[:, g * HD:(g + 1) * HD] = (o[:, :HD] / o[:, HD:]).astype(jnp.bfloat16)


MESH = pl.DeviceIdType.MESH
CUT = 104
NY = 4
NZ = 8


def forward_rules():
    rules = {}
    todo = [("B", 0, 0, None), ("A", 0, 0, None)]
    while todo:
        piece = todo.pop(0)
        if piece in rules:
            continue
        part, oy, oz, half = piece
        sends = []

        def go(axis, at, edge, way, name):
            side = 0 if way > 0 else 1
            if abs(at) < edge:
                sends.append((axis, way, name(at - way, half)))
            elif half is None or half == side:
                sends.append((axis, way, name(edge + 1, side)))

        def along_z(way):
            go("z", oz, 3, way, lambda at, h: (part, oy, at, h))

        def along_y(way):
            go("y", oy, 1, way, lambda at, h: (part, at, oz, h))

        first, first_at, first_edge, second, second_at = (
            (along_y, oy, 2, along_z, oz) if part == "A" else (along_z, oz, 4, along_y, oy))
        second_edge = 4 if part == "A" else 2
        if second_at == 0:
            if first_at == 0:
                first(1), first(-1)
            elif first_at != first_edge:
                first(1 if first_at < 0 else -1)
            second(1), second(-1)
        elif second_at != second_edge:
            second(1 if second_at < 0 else -1)
        rules[piece] = sends
        todo += [send[2] for send in sends]
    return rules


def arrival_order(rules):
    size = {"A": CUT, "B": BLOCK - CUT}
    free, order, count = {}, [], 2
    events = [(0.0, 0, ("B", 0, 0, None)), (0.0, 1, ("A", 0, 0, None))]
    while events:
        events.sort()
        now, _, piece = events.pop(0)
        order.append(piece)
        for axis, way, sent in rules[piece]:
            rows = size[sent[0]] * (1.0 if sent[3] is None else 0.5)
            done = max(now, free.get((axis, way), 0.0)) + rows
            free[axis, way] = done
            events.append((done + 38.0, count, sent))
            count += 1
    return order


RULES = forward_rules()
ORDER = arrival_order(RULES)
FAR = [p for p in ORDER if p[1:3] != (0, 0)]
SLOT = {p: i for i, p in enumerate(FAR)}
NEAR = {("y", 1): 0, ("y", -1): 1, ("z", 1): 2, ("z", -1): 3}
FIRST = [("z", 1, "B"), ("z", -1, "B"), ("y", 1, "A"), ("y", -1, "A"), ("z", 1, "A"), ("z", -1, "A"), ("y", 1, "B"), ("y", -1, "B")]


def gather_kernel(kvh, qh, kv, q, send, recv, send_core, recv_core, send1, recv1, send_own, recv_own, sendx, recvx, local):
    seq = lax.axis_index("seq")
    x = lax.axis_index("head")
    core = lax.rem(seq, 2)
    z = lax.rem(seq // 2, NZ)
    y = seq // (2 * NZ)

    def at(oy, oz, c):
        return (lax.rem(y + (oy + NY), NY) * NZ + lax.rem(z + (oz + NZ), NZ)) * 2 + c

    where = {("y", 1): at(1, 0, core), ("y", -1): at(-1, 0, core), ("z", 1): at(0, 1, core), ("z", -1): at(0, -1, core)}
    sibling = at(0, 0, 1 - core)
    barrier = pltpu.get_barrier_semaphore()
    for target in list(where.values()) + [sibling]:
        pl.semaphore_signal(barrier, inc=1, device_id={"seq": target, "head": x}, device_id_type=MESH)
    for r in (1, 2, 3):
        pl.semaphore_signal(barrier, inc=1, device_id={"seq": seq, "head": lax.rem(x + r, 4)}, device_id_type=MESH)
    own_kv = pltpu.make_async_copy(kvh.at[x], kv.at[seq * 4 + x], local.at[0])
    own_q = pltpu.make_async_copy(qh.at[x], q.at[x], local.at[1])
    own_kv.start()
    own_q.start()
    pl.semaphore_wait(barrier, 8)

    def remote(src, dst, s, r, target, head):
        return pltpu.make_async_remote_copy(src_ref=src, dst_ref=dst, send_sem=s, recv_sem=r,
                                            device_id={"seq": target, "head": head}, device_id_type=MESH)

    everything = []

    def x_copy(source, target, which, r):
        to = lax.rem(x + r, 4)
        return remote(source.at[to], target, sendx.at[which, r], recvx.at[which, r], seq, to)

    kv_x = {r: x_copy(kvh, kv.at[seq * 4 + x], 0, r) for r in (1, 3, 2)}
    q_x = {r: x_copy(qh, q.at[x], 1, r) for r in (1, 3, 2)}
    for r in (1, 3, 2):
        kv_x[r].start()

    def rows(part):
        return pl.ds(0, CUT) if part == "A" else pl.ds(CUT, BLOCK - CUT)

    def first_copy(axis, way, part, r):
        block = kv.at[seq * 4 + lax.rem(x + 4 - r, 4), rows(part)]
        i = NEAR[axis, way]
        p = 0 if part == "A" else 1
        return remote(block, block, send1.at[i, p, r], recv1.at[i, p, r], where[axis, way], x)

    def own_copy(r):
        block = kv.at[seq * 4 + lax.rem(x + 4 - r, 4)]
        return remote(block, block, send_own.at[r], recv_own.at[r], sibling, x)

    def piece_ref(piece, c):
        part, oy, oz, half = piece
        start, count = (0, 4) if half is None else (2 * half, 2)
        return kv.at[pl.ds(at(oy, oz, c) * 4 + start, count), rows(part)]

    def far_copy(held, axis, way, sent):
        part, oy, oz, half = sent
        mine = (part, held[1], held[2], half)
        ref = piece_ref(mine, core)
        i = SLOT[sent]
        return remote(ref, ref, send.at[i], recv.at[i], where[axis, way], x)

    def core_copy(piece):
        ref = piece_ref(piece, core)
        i = SLOT[piece]
        return remote(ref, ref, send_core.at[i], recv_core.at[i], sibling, x)

    for r in (0, 1, 3, 2):
        if r == 0:
            own_kv.wait()
        else:
            kv_x[r].wait_recv()
        for axis, way, part in FIRST:
            copy = first_copy(axis, way, part, r)
            copy.start()
            everything.append(copy)
        copy = own_copy(r)
        copy.start()
        everything.append(copy)
        if r == 0:
            for k in (1, 3, 2):
                q_x[k].start()

    for piece in FAR:
        part, oy, oz, half = piece
        if half is None and abs(oy) + abs(oz) == 1:
            axis, way = ("y", -oy) if oy else ("z", -oz)
            for r in (0, 1, 3, 2):
                first_copy(axis, way, part, r).wait_recv()
        else:
            ref = piece_ref(piece, core)
            i = SLOT[piece]
            remote(ref, ref, send.at[i], recv.at[i], sibling, x).wait_recv()
        for axis, way, sent in RULES[piece]:
            copy = far_copy(piece, axis, way, sent)
            copy.start()
            everything.append(copy)
        copy = core_copy(piece)
        copy.start()
        everything.append(copy)

    for r in (0, 1, 3, 2):
        block = kv.at[seq * 4 + lax.rem(x + 4 - r, 4)]
        remote(block, block, send_own.at[r], recv_own.at[r], sibling, x).wait_recv()
    for piece in FAR:
        core_copy(piece).wait_recv()
    own_q.wait()
    for r in (1, 3, 2):
        q_x[r].wait_recv()
        q_x[r].wait_send()
        kv_x[r].wait_send()
    for copy in everything:
        copy.wait_send()


def gather(kvh, qh):
    dma = pltpu.SemaphoreType.DMA
    n = len(FAR)
    return pl.pallas_call(
        gather_kernel,
        out_shape=(jax.ShapeDtypeStruct((256, BLOCK, 2 * HD), jnp.bfloat16), jax.ShapeDtypeStruct((4, BLOCK, 4 * HD), jnp.bfloat16)),
        in_specs=[pl.BlockSpec(memory_space=pltpu.VMEM)] * 2,
        out_specs=[pl.BlockSpec(memory_space=pl.ANY)] * 2,
        scratch_shapes=[dma((n,)), dma((n,)), dma((n,)), dma((n,)), dma((4, 2, 4)), dma((4, 2, 4)), dma((4,)), dma((4,)),
                        dma((2, 4)), dma((2, 4)), dma((2,))],
        compiler_params=pltpu.CompilerParams(collective_id=0, has_side_effects=True),
        name="gather",
    )(kvh, qh)


def on_device(queries, key_value, rand_blocks):
    kv_all, q = gather(key_value.transpose(1, 0, 2), queries.transpose(1, 0, 2))
    q = q.reshape(1024, 512)
    seq = lax.axis_index("seq")
    head = lax.axis_index("head")
    blocks = seq * 4 + jnp.arange(4, dtype=jnp.int32)
    flips = jnp.array([0] + [1 << i for i in range(8)], dtype=jnp.int32)
    shared = blocks[:, None] ^ flips[None]
    mine = lax.dynamic_slice(rand_blocks, (seq * 4, head * 4, 0), (4, 4, 3)).reshape(4, 12)
    table = jnp.concatenate([shared, mine], axis=1).reshape(-1).astype(jnp.int32)
    out = pl.pallas_call(
        attend_kernel,
        grid_spec=pltpu.PrefetchScalarGridSpec(
            num_scalar_prefetch=1, grid=(4,),
            in_specs=[pl.BlockSpec((BLOCK, 4 * HD), lambda c, t: (c, 0)),
                      pl.BlockSpec(memory_space=pl.ANY)],
            out_specs=pl.BlockSpec((BLOCK, 4 * HD), lambda c, t: (c, 0)),
            scratch_shapes=[pltpu.VMEM((2, LISTED * BLOCK, HD), jnp.bfloat16),
                            pltpu.VMEM((2, LISTED * BLOCK, 2 * HD), jnp.bfloat16),
                            pltpu.SemaphoreType.DMA((2, 2, LISTED))]),
        out_shape=jax.ShapeDtypeStruct((1024, 512), jnp.bfloat16),
        compiler_params=pltpu.CompilerParams(dimension_semantics=("arbitrary",), vmem_limit_bytes=60 << 20),
        name="attend",
    )(table, q, kv_all)
    return out.reshape(1024, 1, 512)


def solution(mesh):
    in_specs = (P(("seq", "head"), None, None), P(("seq", "head"), None, None), P())
    return jax.shard_map(on_device, mesh=mesh, in_specs=in_specs, out_specs=P("seq", "head", None), check_vma=False)
```

```python
import jax
import jax.numpy as jnp
import numpy as np
from jax import lax
from jax.experimental import pallas as pl
from jax.experimental.pallas import tpu as pltpu
from jax.sharding import PartitionSpec as P

HD = 128
BLOCK = 256
LATE = 13
NEARBY = 8
FACTOR = HD ** (-0.5) * np.log2(np.e)
NT = (((1,), (1,)), ((), ()))


def softmax_terms(scores, values):
    top = scores[0].max(axis=-1, keepdims=True)
    for part in scores[1:]:
        top = jnp.maximum(top, part.max(axis=-1, keepdims=True))
    total = None
    for part, value in zip(scores, values):
        weights = jnp.exp2((part - top) * FACTOR).astype(jnp.bfloat16)
        term = jnp.dot(weights, value, preferred_element_type=jnp.float32)
        total = term if total is None else total + term
    return top, total


def last_kernel(table, q_ref, mean_ref, log_ref, kv_ref, o_ref, kbuf, vbuf, sem):
    c = pl.program_id(0)
    slot = c % 2

    def copies(step, where):
        made = []
        for j in range(LATE):
            block = table[step * LATE + j]
            made.append(pltpu.make_async_copy(
                kv_ref.at[block, :, 0:HD], kbuf.at[where, pl.ds(j * BLOCK, BLOCK)], sem.at[where, 0, j]))
            made.append(pltpu.make_async_copy(
                kv_ref.at[block, :, HD:2 * HD], vbuf.at[where, pl.ds(j * BLOCK, BLOCK), 0:HD], sem.at[where, 1, j]))
        return made

    @pl.when(c == 0)
    def _():
        for copy in copies(0, 0):
            copy.start()
        vbuf[:, :, HD:2 * HD] = jnp.ones((2, LATE * BLOCK, HD), jnp.bfloat16)

    @pl.when(c + 1 < pl.num_programs(0))
    def _():
        for copy in copies(c + 1, 1 - slot):
            copy.start()

    for copy in copies(c, slot):
        copy.wait()
    for g in range(4):
        lanes = slice(g * HD, (g + 1) * HD)
        q = q_ref[:, lanes]
        spans = [slice(0, BLOCK), slice((1 + 3 * g) * BLOCK, (4 + 3 * g) * BLOCK)]
        scores = [lax.dot_general(q, kbuf[slot, span], NT, preferred_element_type=jnp.float32) for span in spans]
        top, total = softmax_terms(scores, [vbuf[slot, span] for span in spans])
        early = log_ref[:, lanes]
        top = top * FACTOR
        highest = jnp.maximum(early, top)
        keep = jnp.exp2(early - highest)
        add = jnp.exp2(top - highest)
        out = (keep * mean_ref[:, lanes] + add * total[:, :HD]) / (keep + add * total[:, HD:])
        o_ref[:, lanes] = out.astype(jnp.bfloat16)


MESH = pl.DeviceIdType.MESH
CUT = 104
NY = 4
NZ = 8


def forward_rules():
    rules = {}
    todo = [("B", 0, 0, None), ("A", 0, 0, None)]
    while todo:
        piece = todo.pop(0)
        if piece in rules:
            continue
        part, oy, oz, half = piece
        sends = []

        def go(axis, at, edge, way, name):
            side = 0 if way > 0 else 1
            if abs(at) < edge:
                sends.append((axis, way, name(at - way, half)))
            elif half is None or half == side:
                sends.append((axis, way, name(edge + 1, side)))

        def along_z(way):
            go("z", oz, 3, way, lambda at, h: (part, oy, at, h))

        def along_y(way):
            go("y", oy, 1, way, lambda at, h: (part, at, oz, h))

        first, first_at, first_edge, second, second_at = (
            (along_y, oy, 2, along_z, oz) if part == "A" else (along_z, oz, 4, along_y, oy))
        second_edge = 4 if part == "A" else 2
        if second_at == 0:
            if first_at == 0:
                first(1), first(-1)
            elif first_at != first_edge:
                first(1 if first_at < 0 else -1)
            second(1), second(-1)
        elif second_at != second_edge:
            second(1 if second_at < 0 else -1)
        rules[piece] = sends
        todo += [send[2] for send in sends]
    return rules


def arrival_order(rules):
    size = {"A": CUT, "B": BLOCK - CUT}
    free, order, count = {}, [], 2
    events = [(0.0, 0, ("B", 0, 0, None)), (0.0, 1, ("A", 0, 0, None))]
    while events:
        events.sort()
        now, _, piece = events.pop(0)
        order.append(piece)
        for axis, way, sent in rules[piece]:
            rows = size[sent[0]] * (1.0 if sent[3] is None else 0.5)
            done = max(now, free.get((axis, way), 0.0)) + rows
            free[axis, way] = done
            events.append((done + 38.0, count, sent))
            count += 1
    return order


RULES = forward_rules()
ORDER = arrival_order(RULES)
FAR = [p for p in ORDER if p[1:3] != (0, 0)]
SLOT = {p: i for i, p in enumerate(FAR)}
NEAR = {("y", 1): 0, ("y", -1): 1, ("z", 1): 2, ("z", -1): 3}
FIRST = [("z", 1, "B"), ("z", -1, "B"), ("y", 1, "A"), ("y", -1, "A"), ("z", 1, "A"), ("z", -1, "A"), ("y", 1, "B"), ("y", -1, "B")]


NEEDED = [p for p in FAR if p[1:3] in ((0, 1), (0, -1), (0, 2), (0, -2), (1, 0), (-1, 0), (2, 0))]
READY = max(FAR.index(p) for p in NEEDED)
PACE = 6


def gather_kernel(kvh, qh, kv, q, mean, log, send, recv, send_core, recv_core, send1, recv1, send_own, recv_own, sendx, recvx, local,
                  qv, kbuf, vbuf, means, logs, load, store):
    seq = lax.axis_index("seq")
    x = lax.axis_index("head")
    core = lax.rem(seq, 2)
    z = lax.rem(seq // 2, NZ)
    y = seq // (2 * NZ)

    def at(oy, oz, c):
        return (lax.rem(y + (oy + NY), NY) * NZ + lax.rem(z + (oz + NZ), NZ)) * 2 + c

    where = {("y", 1): at(1, 0, core), ("y", -1): at(-1, 0, core), ("z", 1): at(0, 1, core), ("z", -1): at(0, -1, core)}
    sibling = at(0, 0, 1 - core)
    barrier = pltpu.get_barrier_semaphore()
    for target in list(where.values()) + [sibling]:
        pl.semaphore_signal(barrier, inc=1, device_id={"seq": target, "head": x}, device_id_type=MESH)
    for r in (1, 2, 3):
        pl.semaphore_signal(barrier, inc=1, device_id={"seq": seq, "head": lax.rem(x + r, 4)}, device_id_type=MESH)
    own_kv = pltpu.make_async_copy(kvh.at[x], kv.at[seq * 4 + x], local.at[0])
    own_q = pltpu.make_async_copy(qh.at[x], qv.at[x], local.at[1])
    own_kv.start()
    own_q.start()
    pl.semaphore_wait(barrier, 8)

    def remote(src, dst, s, r, target, head):
        return pltpu.make_async_remote_copy(src_ref=src, dst_ref=dst, send_sem=s, recv_sem=r,
                                            device_id={"seq": target, "head": head}, device_id_type=MESH)

    everything = []

    def x_copy(source, target, which, r):
        to = lax.rem(x + r, 4)
        return remote(source.at[to], target, sendx.at[which, r], recvx.at[which, r], seq, to)

    kv_x = {r: x_copy(kvh, kv.at[seq * 4 + x], 0, r) for r in (1, 3, 2)}
    q_x = {r: x_copy(qh, qv.at[x], 1, r) for r in (1, 3, 2)}
    for r in (1, 3, 2):
        kv_x[r].start()

    def rows(part):
        return pl.ds(0, CUT) if part == "A" else pl.ds(CUT, BLOCK - CUT)

    def first_copy(axis, way, part, r):
        block = kv.at[seq * 4 + lax.rem(x + 4 - r, 4), rows(part)]
        i = NEAR[axis, way]
        p = 0 if part == "A" else 1
        return remote(block, block, send1.at[i, p, r], recv1.at[i, p, r], where[axis, way], x)

    def own_copy(r):
        block = kv.at[seq * 4 + lax.rem(x + 4 - r, 4)]
        return remote(block, block, send_own.at[r], recv_own.at[r], sibling, x)

    def piece_ref(piece, c):
        part, oy, oz, half = piece
        start, count = (0, 4) if half is None else (2 * half, 2)
        return kv.at[pl.ds(at(oy, oz, c) * 4 + start, count), rows(part)]

    def far_copy(held, axis, way, sent):
        part, oy, oz, half = sent
        mine = (part, held[1], held[2], half)
        ref = piece_ref(mine, core)
        i = SLOT[sent]
        return remote(ref, ref, send.at[i], recv.at[i], where[axis, way], x)

    def core_copy(piece):
        ref = piece_ref(piece, core)
        i = SLOT[piece]
        return remote(ref, ref, send_core.at[i], recv_core.at[i], sibling, x)

    for r in (0, 1, 3, 2):
        if r == 0:
            own_kv.wait()
        else:
            kv_x[r].wait_recv()
        for axis, way, part in FIRST:
            copy = first_copy(axis, way, part, r)
            copy.start()
            everything.append(copy)
        copy = own_copy(r)
        copy.start()
        everything.append(copy)
        if r == 0:
            for k in (1, 3, 2):
                q_x[k].start()

    vbuf[:, :, HD:2 * HD] = jnp.ones((4, NEARBY * BLOCK, HD), jnp.bfloat16)

    def flip(i, bit):
        return i + bit - 2 * bit * lax.rem(i // bit, 2)

    holders = [seq, sibling, (y * NZ + flip(z, 1)) * 2 + core, (y * NZ + flip(z, 2)) * 2 + core,
               (flip(y, 1) * NZ + z) * 2 + core, (flip(y, 2) * NZ + z) * 2 + core]

    def loads():
        made = []
        for c in range(4):
            blocks = [seq * 4 + c, seq * 4 + (c ^ 1), seq * 4 + (c ^ 2)] + [h * 4 + c for h in holders[1:]]
            for j, block in enumerate(blocks):
                made.append(pltpu.make_async_copy(kv.at[block, :, 0:HD], kbuf.at[c, pl.ds(j * BLOCK, BLOCK)], load.at[c, j, 0]))
                made.append(pltpu.make_async_copy(
                    kv.at[block, :, HD:2 * HD], vbuf.at[c, pl.ds(j * BLOCK, BLOCK), 0:HD], load.at[c, j, 1]))
        return made

    def attend(i, _):
        c = i // 4
        lanes = pl.ds(pl.multiple_of(lax.rem(i, 4) * HD, HD), HD)
        scores = lax.dot_general(qv[c, :, lanes], kbuf[c], NT, preferred_element_type=jnp.float32)
        top, total = softmax_terms([scores], [vbuf[c]])
        sums = total[:, HD:]
        means[c, :, lanes] = total[:, :HD] / sums
        logs[c, :, lanes] = top * FACTOR + jnp.log2(sums)
        return 0

    def results(c):
        return [pltpu.make_async_copy(means.at[c], mean.at[c], store.at[0, c]),
                pltpu.make_async_copy(logs.at[c], log.at[c], store.at[1, c])]

    q_out = pltpu.make_async_copy(qv, q, local.at[2])

    def beside(step):
        if step == READY:
            for r in (0, 1, 3, 2):
                own_copy_in(r).wait_recv()
            for copy in loads():
                copy.start()
            own_q.wait()
            for r in (1, 3, 2):
                q_x[r].wait_recv()
            q_out.start()
        turn, phase = divmod(step - READY - 3, PACE)
        if phase == 0 and 0 <= turn < 8:
            if turn == 0:
                for copy in loads():
                    copy.wait()
            lax.fori_loop(2 * turn, 2 * turn + 2, attend, 0)
            if turn % 2:
                for copy in results(turn // 2):
                    copy.start()

    def own_copy_in(r):
        block = kv.at[seq * 4 + lax.rem(x + 4 - r, 4)]
        return remote(block, block, send_own.at[r], recv_own.at[r], sibling, x)

    for step, piece in enumerate(FAR):
        part, oy, oz, half = piece
        if half is None and abs(oy) + abs(oz) == 1:
            axis, way = ("y", -oy) if oy else ("z", -oz)
            for r in (0, 1, 3, 2):
                first_copy(axis, way, part, r).wait_recv()
        else:
            ref = piece_ref(piece, core)
            i = SLOT[piece]
            remote(ref, ref, send.at[i], recv.at[i], sibling, x).wait_recv()
        for axis, way, sent in RULES[piece]:
            copy = far_copy(piece, axis, way, sent)
            copy.start()
            everything.append(copy)
        copy = core_copy(piece)
        copy.start()
        everything.append(copy)
        beside(step)

    for piece in FAR:
        core_copy(piece).wait_recv()
    q_out.wait()
    for c in range(4):
        for copy in results(c):
            copy.wait()
    for r in (1, 3, 2):
        q_x[r].wait_send()
        kv_x[r].wait_send()
    for copy in everything:
        copy.wait_send()


def gather(kvh, qh):
    dma = pltpu.SemaphoreType.DMA
    n = len(FAR)
    state = jax.ShapeDtypeStruct((4, BLOCK, 4 * HD), jnp.float32)
    return pl.pallas_call(
        gather_kernel,
        out_shape=(jax.ShapeDtypeStruct((256, BLOCK, 2 * HD), jnp.bfloat16), jax.ShapeDtypeStruct((4, BLOCK, 4 * HD), jnp.bfloat16),
                   state, state),
        in_specs=[pl.BlockSpec(memory_space=pltpu.VMEM)] * 2,
        out_specs=[pl.BlockSpec(memory_space=pl.ANY)] * 4,
        scratch_shapes=[dma((n,)), dma((n,)), dma((n,)), dma((n,)), dma((4, 2, 4)), dma((4, 2, 4)), dma((4,)), dma((4,)),
                        dma((2, 4)), dma((2, 4)), dma((3,)),
                        pltpu.VMEM((4, BLOCK, 4 * HD), jnp.bfloat16),
                        pltpu.VMEM((4, NEARBY * BLOCK, HD), jnp.bfloat16),
                        pltpu.VMEM((4, NEARBY * BLOCK, 2 * HD), jnp.bfloat16),
                        pltpu.VMEM((4, BLOCK, 4 * HD), jnp.float32),
                        pltpu.VMEM((4, BLOCK, 4 * HD), jnp.float32),
                        dma((4, NEARBY, 2)), dma((2, 4))],
        compiler_params=pltpu.CompilerParams(collective_id=0, has_side_effects=True),
        name="gather",
    )(kvh, qh)


def on_device(queries, key_value, rand_blocks):
    kv_all, q, mean, log = gather(key_value.transpose(1, 0, 2), queries.transpose(1, 0, 2))
    rows = [a.reshape(4 * BLOCK, 4 * HD) for a in (q, mean, log)]
    seq = lax.axis_index("seq")
    head = lax.axis_index("head")
    blocks = ((seq + 8 - 16 * ((seq // 8) % 2)) * 4 + jnp.arange(4, dtype=jnp.int32)).astype(jnp.int32)
    mine = lax.dynamic_slice(rand_blocks, (seq * 4, head * 4, 0), (4, 4, 3)).reshape(4, 12)
    table = jnp.concatenate([blocks[:, None], mine], axis=1).reshape(-1)
    rows_of = pl.BlockSpec((BLOCK, 4 * HD), lambda c, t: (c, 0))
    out = pl.pallas_call(
        last_kernel,
        grid_spec=pltpu.PrefetchScalarGridSpec(
            num_scalar_prefetch=1, grid=(4,),
            in_specs=[rows_of, rows_of, rows_of, pl.BlockSpec(memory_space=pl.ANY)],
            out_specs=rows_of,
            scratch_shapes=[pltpu.VMEM((2, LATE * BLOCK, HD), jnp.bfloat16),
                            pltpu.VMEM((2, LATE * BLOCK, 2 * HD), jnp.bfloat16),
                            pltpu.SemaphoreType.DMA((2, 2, LATE))]),
        out_shape=jax.ShapeDtypeStruct((4 * BLOCK, 4 * HD), jnp.bfloat16),
        compiler_params=pltpu.CompilerParams(dimension_semantics=("arbitrary",), vmem_limit_bytes=60 << 20),
        name="attend",
    )(table, *rows, kv_all)
    return out.reshape(4 * BLOCK, 1, 4 * HD)


def solution(mesh):
    in_specs = (P(("seq", "head"), None, None), P(("seq", "head"), None, None), P())
    return jax.shard_map(on_device, mesh=mesh, in_specs=in_specs, out_specs=P("seq", "head", None), check_vma=False)
```

```python
import jax
import jax.numpy as jnp
import numpy as np
from jax import lax
from jax.experimental import pallas as pl
from jax.experimental.pallas import tpu as pltpu
from jax.sharding import PartitionSpec as P

HD = 128
BLOCK = 256
LATE = 12
NEARBY = 9
FACTOR = HD ** (-0.5) * np.log2(np.e)
NT = (((1,), (1,)), ((), ()))


def softmax_terms(scores, values):
    top = scores[0].max(axis=-1, keepdims=True)
    for part in scores[1:]:
        top = jnp.maximum(top, part.max(axis=-1, keepdims=True))
    total = None
    for part, value in zip(scores, values):
        weights = jnp.exp2((part - top) * FACTOR).astype(jnp.bfloat16)
        term = jnp.dot(weights, value, preferred_element_type=jnp.float32)
        total = term if total is None else total + term
    return top, total


def last_kernel(table, q_ref, mean_ref, log_ref, kv_ref, o_ref, kbuf, vbuf, sem):
    c = pl.program_id(0)
    slot = c % 2

    def copies(step, where):
        made = []
        for j in range(LATE):
            block = table[step * LATE + j]
            made.append(pltpu.make_async_copy(
                kv_ref.at[block, :, 0:HD], kbuf.at[where, pl.ds(j * BLOCK, BLOCK)], sem.at[where, 0, j]))
            made.append(pltpu.make_async_copy(
                kv_ref.at[block, :, HD:2 * HD], vbuf.at[where, pl.ds(j * BLOCK, BLOCK), 0:HD], sem.at[where, 1, j]))
        return made

    @pl.when(c == 0)
    def _():
        for copy in copies(0, 0):
            copy.start()
        vbuf[:, :, HD:2 * HD] = jnp.ones((2, LATE * BLOCK, HD), jnp.bfloat16)

    @pl.when(c + 1 < pl.num_programs(0))
    def _():
        for copy in copies(c + 1, 1 - slot):
            copy.start()

    for copy in copies(c, slot):
        copy.wait()
    for g in range(4):
        lanes = slice(g * HD, (g + 1) * HD)
        q = q_ref[:, lanes]
        spans = [slice(3 * g * BLOCK, (3 + 3 * g) * BLOCK)]
        scores = [lax.dot_general(q, kbuf[slot, span], NT, preferred_element_type=jnp.float32) for span in spans]
        top, total = softmax_terms(scores, [vbuf[slot, span] for span in spans])
        early = log_ref[:, lanes]
        top = top * FACTOR
        highest = jnp.maximum(early, top)
        keep = jnp.exp2(early - highest)
        add = jnp.exp2(top - highest)
        out = (keep * mean_ref[:, lanes] + add * total[:, :HD]) / (keep + add * total[:, HD:])
        o_ref[:, lanes] = out.astype(jnp.bfloat16)


MESH = pl.DeviceIdType.MESH
NY = 4
NZ = 8


def forward_rules():
    rules = {}
    todo = [(0, 0, None)]
    while todo:
        piece = todo.pop(0)
        if piece in rules:
            continue
        oy, oz, half = piece
        sends = []
        for way in (1, -1):
            side = 0 if way > 0 else 1
            if oz == 0 and oy == 0:
                sends.append(("z", way, (0, -way, None)))
                sends.append(("y", way, (-way, 0, None)))
            elif oz == 0 and oy == -way:
                sends.append(("y", way, (2, 0, side)))
            elif oz == 0 and oy == 2:
                sends.append(("z", way, (2, -way, half)))
            elif oz * way < 0 and abs(oz) < 3:
                sends.append(("z", way, (oy, oz - way, half)))
            elif oz == -3 * way and oy == 0:
                sends.append(("z", way, (0, 4, side)))
        rules[piece] = sends
        todo += [send[2] for send in sends]
    return rules


def arrival_order(rules):
    free, order, count = {}, [], 1
    events = [(0.0, 0, (0, 0, None))]
    while events:
        events.sort()
        now, _, piece = events.pop(0)
        order.append((piece, now))
        for axis, way, sent in rules[piece]:
            done = max(now, free.get((axis, way), 0.0)) + (BLOCK if sent[2] is None else BLOCK // 2)
            free[axis, way] = done
            events.append((done + 40.0, count, sent))
            count += 1
        if piece[0] == 0:
            for way in (1, -1):
                free["y", way] = max(now, free.get(("y", way), 0.0)) + (BLOCK // 2 if piece[2] is None else BLOCK // 4)
    return order


RULES = forward_rules()
TIMES = arrival_order(RULES)
FAR = [p for p, _ in TIMES if p[:2] != (0, 0)]
SLOT = {p: i for i, p in enumerate(FAR)}
FULL = [p for p in FAR if p[0] in (0, 2)]
NEAR = {("y", 1): 0, ("y", -1): 1, ("z", 1): 2, ("z", -1): 3}
OFFSETS = (0, 1, -1, 2, -2, 3, -3, 4)
PICKS = [(oz, step, other) for oz in OFFSETS for step in ((1, -1, 2) if oz == 4 else (1, -1)) for other in (1, 0)
         if (oz, other) != (0, 0)]
NEEDED = [p for p in FAR if p[:2] in ((0, 1), (0, -1), (0, 2), (0, -2), (0, 4), (1, 0), (-1, 0), (2, 0))]
READY = max(FAR.index(p) for p in NEEDED)


def gather_kernel(want, kvh, qh, kv, q, mean, log, send, recv, send_core, recv_core, send1, recv1, send_own, recv_own, sendx, recvx, local,
                  qv, kbuf, vbuf, means, logs, load, store, stage, send_pick, recv_pick, take, *held):
    seq = lax.axis_index("seq")
    x = lax.axis_index("head")
    core = lax.rem(seq, 2)
    z = lax.rem(seq // 2, NZ)
    y = seq // (2 * NZ)

    def at(oy, oz, c):
        return (lax.rem(y + (oy + NY), NY) * NZ + lax.rem(z + (oz + NZ), NZ)) * 2 + c

    where = {("y", 1): at(1, 0, core), ("y", -1): at(-1, 0, core), ("z", 1): at(0, 1, core), ("z", -1): at(0, -1, core)}
    sibling = at(0, 0, 1 - core)
    barrier = pltpu.get_barrier_semaphore()
    others = list(where.values()) + [sibling, at(2, 0, core)] + [at(oy, 0, 1 - core) for oy in (1, -1, 2)]
    for target in others:
        pl.semaphore_signal(barrier, inc=1, device_id={"seq": target, "head": x}, device_id_type=MESH)
    for r in (1, 2, 3):
        pl.semaphore_signal(barrier, inc=1, device_id={"seq": seq, "head": lax.rem(x + r, 4)}, device_id_type=MESH)
    own_kv = pltpu.make_async_copy(kvh.at[x], kv.at[seq * 4 + x], local.at[0])
    own_q = pltpu.make_async_copy(qh.at[x], qv.at[x], local.at[1])
    own_kv.start()
    own_q.start()
    pl.semaphore_wait(barrier, len(others) + 3)

    def remote(src, dst, s, r, target, head):
        return pltpu.make_async_remote_copy(src_ref=src, dst_ref=dst, send_sem=s, recv_sem=r,
                                            device_id={"seq": target, "head": head}, device_id_type=MESH)

    everything = []

    def begin(copy):
        copy.start()
        everything.append(copy)

    def x_copy(source, target, which, r):
        to = lax.rem(x + r, 4)
        return remote(source.at[to], target, sendx.at[which, r], recvx.at[which, r], seq, to)

    kv_x = {r: x_copy(kvh, kv.at[seq * 4 + x], 0, r) for r in (1, 3, 2)}
    q_x = {r: x_copy(qh, qv.at[x], 1, r) for r in (1, 3, 2)}
    for r in (1, 3, 2):
        kv_x[r].start()

    def own_block(r):
        return kv.at[seq * 4 + lax.rem(x + 4 - r, 4)]

    def first_copy(axis, way, r):
        block = own_block(r)
        i = NEAR[axis, way]
        return remote(block, block, send1.at[i, r], recv1.at[i, r], where[axis, way], x)

    def own_copy(r):
        block = own_block(r)
        return remote(block, block, send_own.at[r], recv_own.at[r], sibling, x)

    def piece_ref(oy, oz, half, c):
        start, count = (0, 4) if half is None else (2 * half, 2)
        return kv.at[pl.ds(at(oy, oz, c) * 4 + start, count)]

    def far_copy(oy, oz, axis, way, sent):
        ref = piece_ref(oy, oz, sent[2], core)
        i = SLOT[sent]
        return remote(ref, ref, send.at[i], recv.at[i], where[axis, way], x)

    def core_copy(piece):
        ref = piece_ref(*piece, core)
        i = SLOT[piece]
        return remote(ref, ref, send_core.at[i], recv_core.at[i], sibling, x)

    def pick_copy(i):
        oz, step, other = PICKS[i]
        reader = at(step, 0, 1 - core if other else core)
        return remote(stage.at[i], kv.at[at(0, oz, core) * 4], send_pick.at[i], recv_pick.at[i], reader, x)

    def pick(oz):
        i = OFFSETS.index(oz)
        copy = pltpu.make_async_copy(piece_ref(0, oz, None, core), held[i], take.at[i])
        copy.start()
        copy.wait()
        mine = [j for j in range(len(PICKS)) if PICKS[j][0] == oz]
        for j in mine:
            _, step, other = PICKS[j]
            reader_core = 1 - core if other else core
            block = want[({1: 0, -1: 16, 2: 32}[step] + i) + reader_core * 8]
            stage[j] = held[i][block]
        for j in mine:
            begin(pick_copy(j))

    vbuf[:, :, HD:2 * HD] = jnp.ones((4, NEARBY * BLOCK, HD), jnp.bfloat16)

    def flip(i, bit):
        return i + bit - 2 * bit * lax.rem(i // bit, 2)

    holders = [seq, sibling, (y * NZ + flip(z, 1)) * 2 + core, (y * NZ + flip(z, 2)) * 2 + core, (y * NZ + flip(z, 4)) * 2 + core,
               (flip(y, 1) * NZ + z) * 2 + core, (flip(y, 2) * NZ + z) * 2 + core]

    def loads():
        made = []
        for c in range(4):
            blocks = [seq * 4 + c, seq * 4 + (c ^ 1), seq * 4 + (c ^ 2)] + [h * 4 + c for h in holders[1:]]
            for j, block in enumerate(blocks):
                made.append(pltpu.make_async_copy(kv.at[block, :, 0:HD], kbuf.at[c, pl.ds(j * BLOCK, BLOCK)], load.at[c, j, 0]))
                made.append(pltpu.make_async_copy(
                    kv.at[block, :, HD:2 * HD], vbuf.at[c, pl.ds(j * BLOCK, BLOCK), 0:HD], load.at[c, j, 1]))
        return made

    def attend(i, _):
        c = i // 4
        lanes = pl.ds(pl.multiple_of(lax.rem(i, 4) * HD, HD), HD)
        scores = lax.dot_general(qv[c, :, lanes], kbuf[c], NT, preferred_element_type=jnp.float32)
        top, total = softmax_terms([scores], [vbuf[c]])
        sums = total[:, HD:]
        means[c, :, lanes] = total[:, :HD] / sums
        logs[c, :, lanes] = top * FACTOR + jnp.log2(sums)
        return 0

    def results(c):
        return [pltpu.make_async_copy(means.at[c], mean.at[c], store.at[0, c]),
                pltpu.make_async_copy(logs.at[c], log.at[c], store.at[1, c])]

    q_out = pltpu.make_async_copy(qv, q, local.at[2])

    def turn(i):
        if i == 0:
            for copy in loads():
                copy.wait()
        lax.fori_loop(2 * i, 2 * i + 2, attend, 0)
        if i % 2:
            for copy in results(i // 2):
                copy.start()

    for r in (0, 1, 3, 2):
        if r == 0:
            own_kv.wait()
        else:
            kv_x[r].wait_recv()
        for axis, way in (("z", 1), ("z", -1), ("y", 1), ("y", -1)):
            begin(first_copy(axis, way, r))
        begin(own_copy(r))
        if r == 0:
            for k in (1, 3, 2):
                q_x[k].start()
    pick(0)

    turns = 0
    for step, piece in enumerate(FAR):
        oy, oz, half = piece
        if half is None and abs(oy) + abs(oz) == 1:
            axis, way = ("y", -oy) if oy else ("z", -oz)
            for r in (0, 1, 3, 2):
                first_copy(axis, way, r).wait_recv()
        else:
            ref = piece_ref(oy, oz, half, core)
            i = SLOT[piece]
            remote(ref, ref, send.at[i], recv.at[i], sibling, x).wait_recv()
        for axis, way, sent in RULES[piece]:
            begin(far_copy(oy, oz, axis, way, sent))
        if piece in FULL:
            begin(core_copy(piece))
        if oy == 0 and (half is None or all(p in FAR[:step + 1] for p in ((0, 4, 0), (0, 4, 1)))):
            pick(oz)
        if step == READY:
            for r in (0, 1, 3, 2):
                own_copy(r).wait_recv()
            for copy in loads():
                copy.start()
            own_q.wait()
            for r in (1, 3, 2):
                q_x[r].wait_recv()
            q_out.start()
        elif step > READY and turns < 8:
            turn(turns)
            turns += 1
    for i in range(turns, 8):
        turn(i)

    for i, (oz, step, other) in enumerate(PICKS):
        ref = kv.at[at(-step, oz, 1 - core if other else core) * 4]
        remote(stage.at[i], ref, send_pick.at[i], recv_pick.at[i], sibling, x).wait_recv()
    for piece in FULL:
        core_copy(piece).wait_recv()
    q_out.wait()
    for c in range(4):
        for copy in results(c):
            copy.wait()
    for r in (1, 3, 2):
        q_x[r].wait_send()
        kv_x[r].wait_send()
    for copy in everything:
        copy.wait_send()


def gather(want, kvh, qh):
    dma = pltpu.SemaphoreType.DMA
    n = len(FAR)
    state = jax.ShapeDtypeStruct((4, BLOCK, 4 * HD), jnp.float32)
    return pl.pallas_call(
        gather_kernel,
        out_shape=(jax.ShapeDtypeStruct((256, BLOCK, 2 * HD), jnp.bfloat16), jax.ShapeDtypeStruct((4, BLOCK, 4 * HD), jnp.bfloat16),
                   state, state),
        in_specs=[pl.BlockSpec(memory_space=pltpu.SMEM)] + [pl.BlockSpec(memory_space=pltpu.VMEM)] * 2,
        out_specs=[pl.BlockSpec(memory_space=pl.ANY)] * 4,
        scratch_shapes=[dma((n,)), dma((n,)), dma((n,)), dma((n,)), dma((4, 4)), dma((4, 4)), dma((4,)), dma((4,)),
                        dma((2, 4)), dma((2, 4)), dma((3,)),
                        pltpu.VMEM((4, BLOCK, 4 * HD), jnp.bfloat16),
                        pltpu.VMEM((4, NEARBY * BLOCK, HD), jnp.bfloat16),
                        pltpu.VMEM((4, NEARBY * BLOCK, 2 * HD), jnp.bfloat16),
                        pltpu.VMEM((4, BLOCK, 4 * HD), jnp.float32),
                        pltpu.VMEM((4, BLOCK, 4 * HD), jnp.float32),
                        dma((4, NEARBY, 2)), dma((2, 4)),
                        pltpu.VMEM((len(PICKS), BLOCK, 2 * HD), jnp.bfloat16), dma((len(PICKS),)), dma((len(PICKS),)), dma((8,))]
        + [pltpu.VMEM((4, BLOCK, 2 * HD), jnp.bfloat16) for _ in OFFSETS],
        compiler_params=pltpu.CompilerParams(collective_id=0, has_side_effects=True),
        name="gather",
    )(want, kvh, qh)


def on_device(queries, key_value, rand_blocks):
    seq = lax.axis_index("seq")
    head = lax.axis_index("head")
    core, z, y = seq % 2, seq // 2 % NZ, seq // (2 * NZ)

    def lists(first, count):
        return lax.dynamic_slice(rand_blocks, (first * 4, head * 4, 0), (count * 4, 4, 3))

    asked = jnp.stack([lists((y + step) % NY * (2 * NZ) + z * 2, 2) for step in (1, 3, 2)]).reshape(3, 2, 1, 48)
    origins = ((y * NZ + (z + np.array(OFFSETS, np.int32) + NZ) % NZ) * 2 + core)[None, None, :, None]
    want = jnp.sum(jnp.where(asked // 4 == origins, asked % 4, 0), axis=-1, dtype=jnp.int32).reshape(-1)
    kv_all, q, mean, log = gather(want, key_value.transpose(1, 0, 2), queries.transpose(1, 0, 2))
    rows = [a.reshape(4 * BLOCK, 4 * HD) for a in (q, mean, log)]
    listed = lists(seq, 1).reshape(48)
    holder = listed // 4
    from_y, from_z = (holder // (2 * NZ) + NY - y) % NY, (holder // 2 % NZ + NZ - z) % NZ
    whole = jnp.where(from_y % 2 == 0, ~((from_y == 2) & (from_z == 4)), (from_z == 0) & (holder % 2 == core))
    table = jnp.where(whole, listed, holder * 4).astype(jnp.int32)
    rows_of = pl.BlockSpec((BLOCK, 4 * HD), lambda c, t: (c, 0))
    out = pl.pallas_call(
        last_kernel,
        grid_spec=pltpu.PrefetchScalarGridSpec(
            num_scalar_prefetch=1, grid=(4,),
            in_specs=[rows_of, rows_of, rows_of, pl.BlockSpec(memory_space=pl.ANY)],
            out_specs=rows_of,
            scratch_shapes=[pltpu.VMEM((2, LATE * BLOCK, HD), jnp.bfloat16),
                            pltpu.VMEM((2, LATE * BLOCK, 2 * HD), jnp.bfloat16),
                            pltpu.SemaphoreType.DMA((2, 2, LATE))]),
        out_shape=jax.ShapeDtypeStruct((4 * BLOCK, 4 * HD), jnp.bfloat16),
        compiler_params=pltpu.CompilerParams(dimension_semantics=("arbitrary",), vmem_limit_bytes=60 << 20),
        name="attend",
    )(table, *rows, kv_all)
    return out.reshape(4 * BLOCK, 1, 4 * HD)


def solution(mesh):
    in_specs = (P(("seq", "head"), None, None), P(("seq", "head"), None, None), P())
    return jax.shard_map(on_device, mesh=mesh, in_specs=in_specs, out_specs=P("seq", "head", None), check_vma=False)
```
